256 devices in a mesh: wide: 64 (over x, y_hi, z), narrow: 4 (over y_lo, core).
Axes of the slice: x: 4, y: 4 (y_hi: 2, y_lo: 2; y = y_hi * 2 + y_lo), z: 8, core: 2. Of those that a mesh axis runs over, the one named last changes fastest.
Arguments:
- constituent_weight_shares: float32 [53, 256, 16, 512], P(None, 'wide', None, 'narrow'), may hold values from 0.05 to 0.5
- normalised_heat_field: float32 [256, 16, 512], P('wide', None, 'narrow'), may hold values from 1 to 2.5
- spreading_rate_table: float32 [53], replicated, may hold values from 0.05 to 0.5
- onward_scale_natlogs: float32 [325], replicated, may hold values from 1 to 4
- onward_thermal_exponent: float32 [325], replicated, may hold values from -1 to 1
- onward_barrier_kelvin: float32 [325], replicated, may hold values from 0.5 to 3
- backward_scale_natlogs: float32 [325], replicated, may hold values from 0 to 3
- backward_barrier_kelvin: float32 [325], replicated, may hold values from 1 to 4
- input_multiplier_matrix: int32 [325, 53], replicated, may hold values from 0 to 2, as said below
- outcome_multiplier_matrix: int32 [325, 53], replicated, may hold values from 0 to 2, as said below
- atom_tally_matrix: int32 [5, 53], replicated, may hold values from 0 to 4
- studied_block_labels: int32 [4096], P(('wide', 'narrow')), may hold values from 0 to 4095, as said below
Outputs:
- section_frac: float32 [53, 256, 16, 512], P(None, 'wide', None, 'narrow')
- path_flux: float32 [4096, 5, 2809], P(('wide', 'narrow'))
The draws below stay inside these ranges and needn't reach their ends.
Inputs may be any that keep to these rules, and one draw needn't show every extreme that they name: `input_multiplier_matrix`: each reaction has two distinct reactant species with coefficient 1 or 2, zeros elsewhere. `outcome_multiplier_matrix`: each reaction has two distinct product species with coefficient 1 or 2, none of them a reactant, zeros elsewhere. `studied_block_labels`: distinct block numbers; of the 16 entries of one device, at most 1 lie in one group of 4 planes (blocks g * 4096 // 256 * 4 up to the next group), and some device has exactly 1 in one group.
All inputs are finite; a program needn't handle non-finite values.
Results may differ from the reference program's by a relative error of at most 0.0003.
Values sent between devices are 32-bit elements; how exact they have to be, the bound alone decides.
A program may use at most 192 MiB of HBM per device.

```python
import math
import jax
import jax.numpy as jnp
from jax import lax

S = 53
NUM_CHEMISTRY = 325
E = 5
GRID_LENGTH_TWO = 16
CZ = 128
BYR = 4
WIN_DEV = 16
GRID_LENGTH_ONE = 256
GRID_LENGTH_THREE = 512
NBLK = 4096
WIN = 4096
N_WIDE = 64
N_NARROW = 4


def stoich_pair(key):
    base = jax.random.fold_in(key, 11)
    keys = jax.random.split(base, NUM_CHEMISTRY)

    def single(reaction_key):
        first_key, second_key = jax.random.split(reaction_key)
        picks = jax.random.permutation(first_key, S)[:4]
        coeffs = jax.random.randint(second_key, (4,), 1, 3)
        table = jax.nn.one_hot(picks, S, dtype=jnp.int32) * coeffs[:, None]
        return (jnp.sum(table[:2], axis=0), jnp.sum(table[2:], axis=0))
    reactants, products = jax.vmap(single)(keys)
    return (reactants.astype(jnp.int32), products.astype(jnp.int32))


def draw_input_multiplier_matrix(key, part):
    return stoich_pair(key)[0]


def draw_outcome_multiplier_matrix(key, part):
    return stoich_pair(key)[1]


def draw_studied_block_labels(key, part):
    first_key, second_key, third_key = jax.random.split(jax.random.fold_in(key, 5), 3)
    analysers = WIN // WIN_DEV
    per_group = NBLK // N_WIDE
    flat = jnp.arange(WIN, dtype=jnp.int32)
    owner = (flat // WIN_DEV).astype(jnp.int32)
    entry = (flat % WIN_DEV).astype(jnp.int32)
    group_map = jax.random.permutation(first_key, N_WIDE).astype(jnp.int32)
    group = jnp.take(group_map, (owner + entry) % N_WIDE)
    order = jnp.argsort(group, stable=True).astype(jnp.int32)
    load = WIN // N_WIDE
    sorted_rank = (jnp.arange(WIN, dtype=jnp.int32) - jnp.take(group, order) * load).astype(jnp.int32)
    rank = jnp.zeros((WIN,), jnp.int32).at[order].set(sorted_rank)
    group_keys = jax.random.split(second_key, N_WIDE)
    tables = jax.vmap(lambda k: jax.random.permutation(k, per_group).astype(jnp.int32))(group_keys)
    chosen = group * per_group + tables[group, rank]
    row_keys = jax.random.split(third_key, analysers)
    shuffles = jax.vmap(lambda k: jax.random.permutation(k, WIN_DEV).astype(jnp.int32))(row_keys)
    rows = chosen.reshape(analysers, WIN_DEV)
    mixed = jnp.take_along_axis(rows, shuffles, axis=1)
    return mixed.reshape(-1).astype(jnp.int32)


def set_ends(array, own_key, least, top_value):
    longest = array.shape.index(max(array.shape))
    spots = []
    for shift in (0, 1):
        where = [jax.random.randint(jax.random.fold_in(own_key, axis), (), 0, length) for axis, length in enumerate(array.shape)]
        where[longest] = (where[longest] + shift) % array.shape[longest]
        spots.append(tuple(where))
    return array.at[spots[0]].set(least).at[spots[1]].set(top_value)


def steps_of(key, extent, cuts, least, high):
    gain, own = 1.0, jax.random.fold_in(key, 6)
    for dim, shards_of in cuts:
        draws = jnp.exp(jax.random.uniform(jax.random.fold_in(own, dim), (shards_of,), jnp.float32, least / len(cuts), high / len(cuts)))
        gain = gain * jnp.repeat(draws, extent[dim] // shards_of).reshape([-1 if axis == dim else 1 for axis in range(len(extent))])
    return gain


def setup_inputs(seed: int = 0) -> dict:
    streams_of = jax.random.split(jax.random.key(seed), 13)
    return {
        "constituent_weight_shares": jnp.clip(jnp.exp(math.log(0.5) - 2.3025851 * jax.random.uniform(streams_of[0], (S, GRID_LENGTH_ONE, GRID_LENGTH_TWO, GRID_LENGTH_THREE), jnp.float32) ** steps_of(streams_of[0], (S, GRID_LENGTH_ONE, GRID_LENGTH_TWO, GRID_LENGTH_THREE), ((1, 64), (3, 4)), -0.2, 0.2)), 0.05, 0.5),
        "normalised_heat_field": jnp.clip(1.0 + 1.5 * jax.random.uniform(streams_of[1], (GRID_LENGTH_ONE, GRID_LENGTH_TWO, GRID_LENGTH_THREE), jnp.float32) ** steps_of(streams_of[1], (GRID_LENGTH_ONE, GRID_LENGTH_TWO, GRID_LENGTH_THREE), ((0, 64), (2, 4)), -0.2, 0.2), 1.0, 2.5),
        "spreading_rate_table": jnp.clip(jnp.exp(jax.random.uniform(streams_of[2], (S,), jnp.float32, math.log(0.05), math.log(0.5))), 0.05, 0.5),
        "onward_scale_natlogs": jnp.clip(jax.random.uniform(streams_of[3], (NUM_CHEMISTRY,), jnp.float32, 1.0, 4.0), 1.0, 4.0),
        "onward_thermal_exponent": jnp.clip(jax.random.uniform(streams_of[4], (NUM_CHEMISTRY,), jnp.float32, -1.0, 1.0), -1.0, 1.0),
        "onward_barrier_kelvin": jnp.clip(jax.random.uniform(streams_of[5], (NUM_CHEMISTRY,), jnp.float32, 0.5, 3.0), 0.5, 3.0),
        "backward_scale_natlogs": jnp.clip(jax.random.uniform(streams_of[6], (NUM_CHEMISTRY,), jnp.float32, 0.0, 3.0), 0.0, 3.0),
        "backward_barrier_kelvin": jnp.clip(jax.random.uniform(streams_of[7], (NUM_CHEMISTRY,), jnp.float32, 1.0, 4.0), 1.0, 4.0),
        "input_multiplier_matrix": draw_input_multiplier_matrix(jax.random.fold_in(streams_of[12], 71), 0),
        "outcome_multiplier_matrix": draw_outcome_multiplier_matrix(jax.random.fold_in(streams_of[12], 71), 0),
        "atom_tally_matrix": set_ends(jax.random.randint(streams_of[10], (E, S), 0, 5), jax.random.fold_in(streams_of[10], 1), 0, 4).astype(jnp.int32),
        "studied_block_labels": draw_studied_block_labels(jax.random.fold_in(streams_of[12], 71), 0),
    }


stencil_weights = (-205.0 / 72.0, 8.0 / 5.0, -1.0 / 5.0, 8.0 / 315.0, -1.0 / 560.0)
section_step = 0.02


def speed_lookup(natural_logarithms, heat_value, onward_factor, backward_factor, onward_scale_natlogs, onward_thermal_exponent, onward_barrier_kelvin, backward_scale_natlogs, backward_barrier_kelvin):
    natural_logheat = jnp.log(heat_value)
    reciprocal_heat = 1.0 / heat_value
    onward_total = jnp.dot(onward_factor, natural_logarithms, precision=lax.Precision.HIGHEST, preferred_element_type=jnp.float32)
    rev_sum = jnp.dot(backward_factor, natural_logarithms, precision=lax.Precision.HIGHEST, preferred_element_type=jnp.float32)
    onward_rate_vector = jnp.exp(onward_scale_natlogs[:, None] + onward_thermal_exponent[:, None] * natural_logheat[None, :] - onward_barrier_kelvin[:, None] * reciprocal_heat[None, :] + onward_total)
    backward = jnp.exp(backward_scale_natlogs[:, None] - backward_barrier_kelvin[:, None] * reciprocal_heat[None, :] + rev_sum)
    return onward_rate_vector - backward


def reference(constituent_weight_shares, normalised_heat_field, spreading_rate_table, onward_scale_natlogs, onward_thermal_exponent, onward_barrier_kelvin, backward_scale_natlogs, backward_barrier_kelvin, input_multiplier_matrix, outcome_multiplier_matrix, atom_tally_matrix, studied_block_labels):
    onward_factor = input_multiplier_matrix.astype(jnp.float32)
    backward_factor = outcome_multiplier_matrix.astype(jnp.float32)
    net_t = (backward_factor - onward_factor).T
    offsets_base = jnp.arange(-4, 5, dtype=jnp.int32)

    def plane_step(leading_offset_index):
        offsets = ((leading_offset_index + offsets_base) % GRID_LENGTH_ONE).astype(jnp.int32)
        stack_x = jnp.take(constituent_weight_shares, offsets, axis=1)
        centre = stack_x[:, 4]
        laplace = 3.0 * stencil_weights[0] * centre
        for shift_by in range(1, 5):
            laplace = laplace + stencil_weights[shift_by] * (
                stack_x[:, 4 + shift_by] + stack_x[:, 4 - shift_by]
                + jnp.roll(centre, shift_by, 1) + jnp.roll(centre, -shift_by, 1)
                + jnp.roll(centre, -shift_by, 2) + jnp.roll(centre, shift_by, 2))
        heat_plane_piece = jnp.take(normalised_heat_field, leading_offset_index, axis=0).reshape(-1)
        natural_logarithms = jnp.log(centre).reshape(S, -1)
        speed_vector = speed_lookup(natural_logarithms, heat_plane_piece, onward_factor, backward_factor, onward_scale_natlogs, onward_thermal_exponent, onward_barrier_kelvin, backward_scale_natlogs, backward_barrier_kelvin)
        production = jnp.dot(net_t, speed_vector, precision=lax.Precision.HIGHEST, preferred_element_type=jnp.float32).reshape(S, GRID_LENGTH_TWO, GRID_LENGTH_THREE)
        fresh = centre + section_step * (spreading_rate_table[:, None, None] * laplace + production)
        sums = speed_vector.reshape(NUM_CHEMISTRY, GRID_LENGTH_TWO // BYR, BYR, N_NARROW, CZ).sum(axis=(2, 4))
        return fresh, jnp.transpose(sums, (1, 2, 0))

    planes_out, block_sums = lax.map(plane_step, jnp.arange(GRID_LENGTH_ONE, dtype=jnp.int32))
    section_frac = jnp.transpose(planes_out, (1, 0, 2, 3))
    block_rates = block_sums.reshape(-1, NUM_CHEMISTRY)
    picked = jnp.take(block_rates, studied_block_labels, axis=0)
    element_f = atom_tally_matrix.astype(jnp.float32)
    results = []
    for element in range(E):
        source = onward_factor * element_f[element][None, :]
        denom = jnp.maximum(jnp.sum(source, axis=1), 1.0)
        source = source / denom[:, None]
        target = backward_factor * element_f[element][None, :]
        pairs = (source[:, :, None] * target[:, None, :]).reshape(NUM_CHEMISTRY, S * S)
        results.append(jnp.dot(picked, pairs, precision=lax.Precision.HIGHEST, preferred_element_type=jnp.float32))
    path_flux = jnp.stack(results, axis=1)
    return section_frac, path_flux
```

```python
import functools

import jax
import jax.numpy as jnp
from jax import lax
from jax.experimental import pallas as pl
from jax.experimental.pallas import tpu as pltpu
from jax.sharding import PartitionSpec as P

MESH = pl.DeviceIdType.MESH
F32, BF16, I32 = jnp.float32, jnp.bfloat16, jnp.int32

S, SP = 53, 56
R, RP, RK = 325, 336, 384
PAIRS, PAIRSP = 2809, 2816
E = 5
NX, NY, NZ = 4, 16, 128
WIDE, NARROW = 64, 4
RING, CROSS = 8, 8
ENTRIES = 16
LOG2E = 1.4426950408889634
TAPS = (-14350.0, 8064.0, -1008.0, 128.0, -9.0)
STEP = 0.02
EARLY = 4
LATE = 4


def split2(v):
    hi = v.astype(BF16)
    return hi, (v - hi.astype(F32)).astype(BF16)


def split3(v):
    hi = v.astype(BF16)
    rest = v - hi.astype(F32)
    mid = rest.astype(BF16)
    return hi, mid, (rest - mid.astype(F32)).astype(BF16)


def iota(shape, dim):
    return lax.broadcasted_iota(I32, shape, dim)


def mm(a, b):
    return jnp.dot(a, b, preferred_element_type=F32)


def mm_t(a, b):
    return lax.dot_general(a, b, (((1,), (1,)), ((), ())), preferred_element_type=F32)


def taps_of(distance):
    w = jnp.zeros(distance.shape, F32)
    for k in range(1, 5):
        w = jnp.where(jnp.abs(distance) == k, TAPS[k], w)
    return w


def kernel(
    c_ref, heat_ref, spread_ref, fs_ref, ft_ref, fb_ref, bs_ref, bb_ref,
    in_ref, out_ref, atom_ref, lab_ref,
    frac_ref, flux_ref,
    ct, lo, hi, base, weights, rhs, rr, net, acc, sums, infull, outfull, atomf,
    spread, mine, lab1, lab2, lab2src, edge, edge_l, edge_r, rows, zsend, zrecv, xsend, xrecv,
    pairs, afac, dens, flux,
    heat_v, v0, v1, v2, v3, v4, vecrows, spread_v, in_v, out_v, atom_v, lab_v,
    load_sem, store_sem, flux_sem, hs_sem, hr_sem, l1s, l1r, l2s, l2r, es, er, ns, nr, zs, zr, xs, xr, small_sem,
):
    vecs = (v0, v1, v2, v3, v4)
    w = lax.axis_index("wide")
    n = lax.axis_index("narrow")
    ring = lax.rem(w, RING)
    cross = w // RING
    right, left = lax.rem(w + 1, WIDE), lax.rem(w + WIDE - 1, WIDE)

    def ring_peer(i):
        return cross * RING + lax.rem(ring + i, RING)

    def cross_peer(i):
        return lax.rem(cross + i, CROSS) * RING + ring

    def narrow_peer(i):
        return lax.rem(n + i, NARROW)

    barrier = pltpu.get_barrier_semaphore()

    def greet(dev):
        pl.semaphore_signal(barrier, inc=1, device_id=dev, device_id_type=MESH)

    greet((right, n))
    greet((left, n))
    for i in range(1, NARROW):
        greet((w, narrow_peer(i)))
    for i in range(1, RING):
        greet((ring_peer(i), n))
    for i in range(1, CROSS):
        greet((cross_peer(i), n))

    def load(y, x):
        return pltpu.make_async_copy(
            c_ref.at[:, x, y, :], ct.at[y, x, pl.ds(0, S)], load_sem.at[y, x]
        )

    @pl.loop(0, NY)
    def _(y):
        for x in range(NX):
            load(y, x).start()

    smalls = [
        pltpu.make_async_copy(a, b, small_sem.at[i])
        for i, (a, b) in enumerate(
            (
                (heat_ref, heat_v), (spread_ref, spread_v), (fs_ref, vecs[0]), (ft_ref, vecs[1]),
                (fb_ref, vecs[2]), (bs_ref, vecs[3]), (bb_ref, vecs[4]),
                (in_ref, in_v), (out_ref, out_v), (atom_ref, atom_v),
            )
        )
    ]
    lab_copy = pltpu.make_async_copy(lab_ref, lab_v, small_sem.at[10])
    lab_copy.start()
    for c in smalls:
        c.start()

    lab_copy.wait()
    mine[...] = jnp.full((8, 128), -1, I32)
    mine[:, 0:ENTRIES] = jnp.broadcast_to(lab_v[...].reshape(1, ENTRIES), (8, ENTRIES))

    ct[:, :, S:SP, :] = jnp.ones((NY, NX, SP - S, NZ), F32)

    @pl.loop(0, NY)
    def _(y):
        for x in range(NX):
            load(y, x).wait()

    pl.semaphore_wait(barrier, 2 + (NARROW - 1) + (RING - 1) + (CROSS - 1))

    def lab1_copy(i):
        return pltpu.make_async_remote_copy(
            mine, lab1.at[cross], l1s.at[i], l1r.at[i],
            device_id=(cross_peer(i), n), device_id_type=MESH,
        )

    for i in range(1, CROSS):
        lab1_copy(i).start()

    def halo_up(k):
        return pltpu.make_async_remote_copy(
            ct.at[k, :, pl.ds(0, S)], lo.at[k, :, pl.ds(0, S)], hs_sem.at[0, k], hr_sem.at[0, k],
            device_id=(right, n), device_id_type=MESH,
        )

    def halo_down(k):
        return pltpu.make_async_remote_copy(
            ct.at[k, :, pl.ds(0, S)], hi.at[k, :, pl.ds(0, S)], hs_sem.at[1, k], hr_sem.at[1, k],
            device_id=(left, n), device_id_type=MESH,
        )

    @pl.loop(0, EARLY)
    def _(k):
        halo_up(k).start()
        halo_down(k).start()

    lane_e = iota((NX * SP, NZ), 1)
    packed = jnp.zeros((NX * SP, NZ), F32)
    for y in range(NY):
        t = ct[y].reshape(NX * SP, NZ)
        packed = jnp.where(lane_e // 8 == y, pltpu.roll(t, 4 + 8 * y, 1), packed)
    edge[...] = packed

    for c in smalls:
        c.wait()
    infull[...] = jnp.zeros((128, RK), F32)
    outfull[...] = jnp.zeros((128, RK), F32)
    atomf[...] = jnp.zeros((8, 128), F32)
    infull[0:S, 0:R] = in_v[...].astype(F32)
    outfull[0:S, 0:R] = out_v[...].astype(F32)
    atomf[0:E, 0:S] = atom_v[...].astype(F32)
    spread[...] = jnp.zeros((8, 128), F32)
    spread[:, 0:S] = jnp.broadcast_to(spread_v[...], (8, S))
    sums[...] = jnp.zeros((RK, 128), F32)

    def edge_right():
        return pltpu.make_async_remote_copy(
            edge, edge_l, es.at[0], er.at[0], device_id=(w, narrow_peer(1)), device_id_type=MESH
        )

    def edge_left():
        return pltpu.make_async_remote_copy(
            edge, edge_r, es.at[1], er.at[1],
            device_id=(w, narrow_peer(NARROW - 1)), device_id_type=MESH,
        )

    edge_right().start()
    edge_left().start()

    net_t = outfull[0:64] - infull[0:64]
    fin = jnp.transpose(infull[...])
    fout = jnp.transpose(outfull[...])
    net[:, 0:RK] = net_t.astype(BF16)
    net[:, RK : 2 * RK] = net_t.astype(BF16)

    sub = iota((8, RK), 0)
    vecrows[...] = jnp.zeros((8, RK), F32)
    for k in range(5):
        vecrows[k : k + 1, 0:R] = vecs[k][...].reshape(1, R)
    vec = vecrows[...]
    scale_of = jnp.where((sub == 1), 1.0, LOG2E)
    cols = jnp.transpose(vec * scale_of)
    lane_w = iota((RP, 128), 1)

    def param_lanes(scale, power, barrier_):
        s3 = split3(scale)
        w_ = jnp.zeros((RP, 128), F32)
        vals = [s.astype(F32) for s in s3]
        if power is not None:
            ph, plo = (v.astype(F32) for v in split2(power))
            vals += [ph, plo, ph]
        else:
            vals += [None] * 3
        bh, bl = (v.astype(F32) for v in split2(barrier_))
        vals += [-bh, -bl, -bh]
        for k, v in enumerate(vals):
            if v is not None:
                w_ = jnp.where(lane_w == k, jnp.broadcast_to(v, (RP, 128)), w_)
        return w_.astype(BF16)

    for at, full, power, s, b in ((0, fin, 1, 0, 2), (RP, fout, None, 3, 4)):
        m = full[0:RP]
        weights[at : at + RP, 0:128] = (m + pltpu.roll(m, 64, 1)).astype(BF16)
        weights[at : at + RP, 128:256] = param_lanes(
            cols[0:RP, s : s + 1],
            None if power is None else cols[0:RP, power : power + 1],
            cols[0:RP, b : b + 1],
        )
    rhs[...] = jnp.zeros((256, NX * NZ), BF16)
    rr[...] = jnp.zeros((2 * RK, NX * NZ), BF16)

    gathered = jnp.zeros((8, 128), I32)
    sub8 = iota((8, 128), 0)
    for i in range(1, CROSS):
        lab1_copy(i).wait()
    lab1[cross] = mine[...]
    for i in range(CROSS):
        gathered = jnp.where(sub8 == i, lab1[i], gathered)
    lab2src[...] = gathered
    lab2[ring] = gathered

    def lab2_copy(i):
        return pltpu.make_async_remote_copy(
            lab2src, lab2.at[ring], l2s.at[i], l2r.at[i],
            device_id=(ring_peer(i), n), device_id_type=MESH,
        )

    spread_col = jnp.transpose(jnp.broadcast_to(spread[0:1], (8, 128)))[0:SP, 0:1]
    spread_b = jnp.broadcast_to(spread_col, (SP, NZ)) * (STEP / 5040.0)

    for i in range(1, RING):
        lab2_copy(i).start()

    sub16 = iota((16, NZ), 0)

    @pl.loop(0, NY // 4)
    def _(g):
        acc[...] = jnp.zeros((RP, NX * NZ), F32)

        @pl.loop(0, 4)
        def _(q):
            y = g * 4 + q

            @pl.when(y + EARLY < NY - LATE)
            def _():
                halo_up(y + EARLY).start()
                halo_down(y + EARLY).start()

            for x in range(NX):
                zs_ = slice(x * NZ, (x + 1) * NZ)
                logs = jnp.log(ct[y, x]) * LOG2E
                h, l = split2(logs)
                rhs[0:SP, zs_] = h
                rhs[64 : 64 + SP, zs_] = l
                t = heat_v[x, pl.ds(y, 1), :]
                lt_h, lt_l = (v.astype(F32) for v in split2(jnp.log(t) * LOG2E))
                it_h, it_l = (v.astype(F32) for v in split2(1.0 / t))
                p = jnp.where(sub16 < 3, 1.0, 0.0)
                for first, vh, vl in ((3, lt_h, lt_l), (6, it_h, it_l)):
                    p = jnp.where((sub16 == first) | (sub16 == first + 1), jnp.broadcast_to(vh, (16, NZ)), p)
                    p = jnp.where(sub16 == first + 2, jnp.broadcast_to(vl, (16, NZ)), p)
                rhs[128:144, zs_] = p.astype(BF16)
            a = mm(weights[...], rhs[...])
            rates = jnp.exp2(a[0:RP]) - jnp.exp2(a[RP : 2 * RP])
            h, l = split2(rates)
            rr[0:RP] = h
            rr[RK : RK + RP] = l
            acc[...] += rates
            prod = mm(net[...], rr[...])
            for x in range(NX):
                base[y, x] = ct[y, x] + STEP * prod[0:SP, x * NZ : (x + 1) * NZ]

        lane_r = iota((RP, 128), 1)
        cur = sums[0:RP]
        for x in range(NX):
            col = jnp.sum(acc[:, x * NZ : (x + 1) * NZ], axis=1, keepdims=True)
            cur = jnp.where(lane_r == x * 4 + g, jnp.broadcast_to(col, (RP, 128)), cur)
        sums[0:RP] = cur

    rows[pl.ds(pl.multiple_of(n * 16, 16), 16), :] = jnp.transpose(sums[...])[0:16]

    for i in range(1, RING):
        lab2_copy(i).wait()

    labels = lab2[...].reshape(RING * CROSS, 128)
    group = lax.shift_right_arithmetic(labels, 6)
    local = jnp.bitwise_and(labels, 63)
    row_of = jnp.bitwise_and(local, 3) * 16 + lax.shift_right_arithmetic(local, 2)
    wanted = jnp.max(jnp.where(group == w, row_of, -1).astype(F32), axis=1, keepdims=True)
    choose = jnp.where(
        jnp.broadcast_to(wanted, (64, 64)) == iota((64, 64), 1).astype(F32), 1.0, 0.0
    ).astype(BF16)

    def rows_copy(i):
        part = rows.at[pl.ds(pl.multiple_of(n * 16, 16), 16)]
        return pltpu.make_async_remote_copy(
            part, part, ns.at[i], nr.at[i], device_id=(w, narrow_peer(i)), device_id_type=MESH
        )

    for i in range(1, NARROW):
        rows_copy(i).start()

    a_h = atomf[...].astype(BF16)
    denom = jnp.maximum(mm_t(a_h, fin.astype(BF16)), 1.0)
    dens[...] = 1.0 / denom
    in_b = fin.astype(BF16)
    out_b = fout.astype(BF16)

    @pl.loop(0, PAIRSP // 256)
    def _(t):
        ij = (iota((128, 256), 1) + t * 256).astype(F32)
        i_of = jnp.floor((ij + 0.5) * (1.0 / 53.0))
        j_of = ij - 53.0 * i_of
        want = iota((128, 256), 0).astype(F32)
        r_ = jnp.where(i_of == want, 1.0, 0.0).astype(BF16)
        q_ = jnp.where(j_of == want, 1.0, 0.0).astype(BF16)
        at = pl.ds(pl.multiple_of(t * 256, 256), 256)
        pairs[:, at] = (mm(in_b, r_) * mm(out_b, q_)).astype(BF16)
        afac[:, at] = mm(a_h, r_) * mm(a_h, q_)

    for i in range(1, NARROW):
        rows_copy(i).wait()

    picked3 = split3(rows[...])
    zsend[...] = sum(mm(choose, p) for p in picked3).reshape(RING, CROSS, RK)
    zrecv[ring] = zsend[ring]

    def ring_copy(i):
        to = lax.rem(ring + i, RING)
        return pltpu.make_async_remote_copy(
            zsend.at[to], zrecv.at[ring], zs.at[i], zr.at[i],
            device_id=(ring_peer(i), n), device_id_type=MESH,
        )

    er_wait = (edge_right(), edge_left())
    for c in er_wait:
        c.wait()

    for i in range(1, RING):
        ring_copy(i).start()

    @pl.loop(NY - LATE, NY)
    def _(k):
        halo_up(k).start()
        halo_down(k).start()

    merged = jnp.where(jnp.bitwise_and(lane_e, 7) < 4, edge_l[...], edge_r[...])
    m_h, m_l = split2(merged)
    zi, zo = iota((NZ, NZ), 0), iota((NZ, NZ), 1)
    band = taps_of(zi - zo).astype(BF16)

    @pl.loop(0, NY)
    def _(y):
        c = ct[y].reshape(NX * SP, NZ)
        c_h, c_l = split2(c)
        slot = zi - 8 * y
        at = jnp.where(slot < 4, slot - 4, NZ + slot - 4)
        side = jnp.where((slot >= 0) & (slot < 8), taps_of(at - zo), 0.0).astype(BF16)
        along = mm(c_h, band) + mm(c_l, band) + mm(m_h, side) + mm(m_l, side)
        for x in range(NX):
            lap = along[x * SP : (x + 1) * SP] + (3.0 * TAPS[0]) * ct[y, x]
            for k in range(1, 5):
                t = ct[lax.rem(y + k, NY), x] + ct[lax.rem(y + NY - k, NY), x]
                if x + k < NX:
                    t = t + ct[y, x + k]
                if x - k >= 0:
                    t = t + ct[y, x - k]
                lap = lap + TAPS[k] * t
            base[y, x] = base[y, x] + spread_b * lap

    for i in range(1, RING):
        ring_copy(i).wait()

    got = zrecv[...]
    sub_k = iota((8, RK), 0)
    for d in range(CROSS):
        out = jnp.zeros((8, RK), F32)
        for z in range(RING):
            out = jnp.where(sub_k == z, jnp.broadcast_to(got[z, d : d + 1], (8, RK)), out)
        xsend[d] = out
    xrecv[cross] = xsend[cross]

    def cross_copy(i):
        to = lax.rem(cross + i, CROSS)
        return pltpu.make_async_remote_copy(
            xsend.at[to], xrecv.at[cross], xs.at[i], xr.at[i],
            device_id=(cross_peer(i), n), device_id_type=MESH,
        )

    entry_tile = jnp.transpose(jnp.broadcast_to(mine[0:1].astype(F32), (8, 128)))[0:ENTRIES, 0:1]
    group_of = jnp.floor(entry_tile * (1.0 / 64.0))
    pick = jnp.where(
        jnp.broadcast_to(group_of, (ENTRIES, 64)) == iota((ENTRIES, 64), 1).astype(F32), 1.0, 0.0
    ).astype(BF16)

    for i in range(1, CROSS):
        cross_copy(i).start()
    for i in range(1, CROSS):
        cross_copy(i).wait()

    picked = sum(mm(pick, p) for p in split3(xrecv[...].reshape(WIDE, RK)))
    scaled = (
        jnp.concatenate(
            [picked * jnp.broadcast_to(dens[k : k + 1], (ENTRIES, RK)) for k in range(E)], axis=0
        )
    )[:, 0:RK]
    s_h, s_l = split2(scaled)
    s_h, s_l = s_h[:, 0:RK], s_l[:, 0:RK]

    for t in range(PAIRSP // 256):
        size = min(256, PAIRS - t * 256)
        at = slice(t * 256, t * 256 + 256)
        v = mm(s_h, pairs[:, at]) + mm(s_l, pairs[:, at])
        for k in range(E):
            f = v[k * ENTRIES : (k + 1) * ENTRIES] * afac[k : k + 1, at]
            flux[k, :, t * 256 : t * 256 + size] = f[:, 0:size]
    flux_copy = pltpu.make_async_copy(flux, flux_ref, flux_sem)
    flux_copy.start()

    def store(y, x):
        return pltpu.make_async_copy(
            base.at[y, x, pl.ds(0, S)], frac_ref.at[:, x, y, :], store_sem.at[y, x]
        )

    @pl.loop(0, NY)
    def _(y):
        halo_up(y).wait()
        halo_down(y).wait()
        for x in range(NX):
            lap = jnp.zeros((SP, NZ), F32)
            for k in range(1, 5):
                if x - k < 0:
                    lap = lap + TAPS[k] * lo[y, NX + x - k]
                if x + k >= NX:
                    lap = lap + TAPS[k] * hi[y, x + k - NX]
            base[y, x] = base[y, x] + spread_b * lap
            store(y, x).start()

    @pl.loop(0, NY)
    def _(y):
        for x in range(NX):
            store(y, x).wait()

    flux_copy.wait()


def body(
    shares, heat, spread, fs, ft, fb, bs, bb, reactants, products, atoms, labels
):
    any_ = pl.BlockSpec(memory_space=pl.ANY)
    hbm = pl.BlockSpec(memory_space=pltpu.HBM)
    dma = pltpu.SemaphoreType.DMA
    field = pltpu.VMEM((NY, NX, SP, NZ), F32)
    scratch = [
        field, field, field, field,
        pltpu.VMEM((2 * RP, 256), BF16),
        pltpu.VMEM((256, NX * NZ), BF16),
        pltpu.VMEM((2 * RK, NX * NZ), BF16),
        pltpu.VMEM((64, 2 * RK), BF16),
        pltpu.VMEM((RP, NX * NZ), F32),
        pltpu.VMEM((RK, 128), F32),
        pltpu.VMEM((128, RK), F32),
        pltpu.VMEM((128, RK), F32),
        pltpu.VMEM((8, 128), F32),
        pltpu.VMEM((8, 128), F32),
        pltpu.VMEM((8, 128), I32),
        pltpu.VMEM((CROSS, 8, 128), I32),
        pltpu.VMEM((RING, 8, 128), I32),
        pltpu.VMEM((8, 128), I32),
        pltpu.VMEM((NX * SP, NZ), F32),
        pltpu.VMEM((NX * SP, NZ), F32),
        pltpu.VMEM((NX * SP, NZ), F32),
        pltpu.VMEM((64, RK), F32),
        pltpu.VMEM((RING, CROSS, RK), F32),
        pltpu.VMEM((RING, CROSS, RK), F32),
        pltpu.VMEM((CROSS, RING, RK), F32),
        pltpu.VMEM((CROSS, RING, RK), F32),
        pltpu.VMEM((RK, PAIRSP), BF16),
        pltpu.VMEM((8, PAIRSP), F32),
        pltpu.VMEM((8, RK), F32),
        pltpu.VMEM((E, ENTRIES, PAIRS), F32),
        pltpu.VMEM((NX, NY, NZ), F32),
        pltpu.VMEM((R,), F32), pltpu.VMEM((R,), F32), pltpu.VMEM((R,), F32), pltpu.VMEM((R,), F32), pltpu.VMEM((R,), F32),
        pltpu.VMEM((8, RK), F32),
        pltpu.VMEM((1, S), F32),
        pltpu.VMEM((S, R), I32),
        pltpu.VMEM((S, R), I32),
        pltpu.VMEM((E, S), I32),
        pltpu.VMEM((ENTRIES,), I32),
        dma((NY, NX)), dma((NY, NX)), dma, dma((2, NY)), dma((2, NY)),
        dma((8,)), dma((8,)), dma((8,)), dma((8,)), dma((2,)), dma((2,)),
        dma((4,)), dma((4,)), dma((8,)), dma((8,)), dma((8,)), dma((8,)), dma((11,)),
    ]
    row = lambda v: v.reshape(1, -1)
    frac, flux = pl.pallas_call(
        kernel,
        out_shape=(
            jax.ShapeDtypeStruct(shares.shape, F32),
            jax.ShapeDtypeStruct((E, ENTRIES, PAIRS), F32),
        ),
        in_specs=[hbm] * 12,
        out_specs=(any_, any_),
        scratch_shapes=scratch,
        compiler_params=pltpu.CompilerParams(
            collective_id=0, has_side_effects=True, vmem_limit_bytes=48 << 20
        ),
    )(
        *(
            pltpu.with_memory_space_constraint(v, pltpu.HBM)
            for v in (
                shares, heat, row(spread), fs, ft, fb, bs, bb, reactants.T, products.T, atoms, labels,
            )
        )
    )
    return frac, jnp.transpose(flux, (1, 0, 2))


def solution(mesh):
    in_specs = (
        P(None, "wide", None, "narrow"), P("wide", None, "narrow"),
        P(), P(), P(), P(), P(), P(), P(), P(), P(), P(("wide", "narrow")),
    )
    out_specs = (P(None, "wide", None, "narrow"), P(("wide", "narrow"), None, None))
    return jax.shard_map(body, mesh=mesh, in_specs=in_specs, out_specs=out_specs, check_vma=False)
```

```python
import functools

import jax
import jax.numpy as jnp
from jax import lax
from jax.experimental import pallas as pl
from jax.experimental.pallas import tpu as pltpu
from jax.sharding import PartitionSpec as P

MESH = pl.DeviceIdType.MESH
F32, BF16, I32 = jnp.float32, jnp.bfloat16, jnp.int32

S, SP = 53, 56
R, RP, RK = 325, 336, 384
PAIRS, PAIRSP = 2809, 2816
E = 5
NX, NY, NZ = 4, 16, 128
WIDE, NARROW = 64, 4
RING, CROSS = 8, 8
ENTRIES = 16
LOG2E = 1.4426950408889634
TAPS = (-14350.0, 8064.0, -1008.0, 128.0, -9.0)
STEP = 0.02
EARLY, EACH, ROWS_AFTER, RING_AFTER = 6, 1, 3, 3
HELD = EARLY + EACH * (NY // 4)
READY = HELD


def split2(v):
    hi = v.astype(BF16)
    return hi, (v - hi.astype(F32)).astype(BF16)


def split3(v):
    hi = v.astype(BF16)
    rest = v - hi.astype(F32)
    mid = rest.astype(BF16)
    return hi, mid, (rest - mid.astype(F32)).astype(BF16)


def iota(shape, dim):
    return lax.broadcasted_iota(I32, shape, dim)


def mm(a, b):
    return jnp.dot(a, b, preferred_element_type=F32)


def mm_t(a, b):
    return lax.dot_general(a, b, (((1,), (1,)), ((), ())), preferred_element_type=F32)


def taps_of(distance):
    w = jnp.zeros(distance.shape, F32)
    for k in range(1, 5):
        w = jnp.where(jnp.abs(distance) == k, TAPS[k], w)
    return w


def kernel(
    c_ref, heat_ref, spread_ref, fs_ref, ft_ref, fb_ref, bs_ref, bb_ref,
    in_ref, out_ref, atom_ref, lab_ref,
    frac_ref, flux_ref,
    ct, lo, hi, base, weights, rhs, rr, net, acc, sums, infull, outfull, atomf,
    spread, mine, lab1, lab2, lab2src, edge, edge_l, edge_r, sides, rows, zsend, zrecv, xsend, xrecv,
    pairs, afac, dens, flux,
    heat_v, v0, v1, v2, v3, v4, vecrows, spread_v, in_v, out_v, atom_v, lab_v,
    load_sem, store_sem, flux_sem, hs_sem, hr_sem, l1s, l1r, l2s, l2r, es, er, ns, nr, zs, zr, xs, xr, small_sem,
):
    vecs = (v0, v1, v2, v3, v4)
    w = lax.axis_index("wide")
    n = lax.axis_index("narrow")
    ring = lax.rem(w, RING)
    cross = w // RING
    right, left = lax.rem(w + 1, WIDE), lax.rem(w + WIDE - 1, WIDE)

    def ring_peer(i):
        return cross * RING + lax.rem(ring + i, RING)

    def cross_peer(i):
        return lax.rem(cross + i, CROSS) * RING + ring

    def narrow_peer(i):
        return lax.rem(n + i, NARROW)

    barrier = pltpu.get_barrier_semaphore()

    def greet(dev):
        pl.semaphore_signal(barrier, inc=1, device_id=dev, device_id_type=MESH)

    greet((right, n))
    greet((left, n))
    for i in range(1, NARROW):
        greet((w, narrow_peer(i)))
    for i in range(1, RING):
        greet((ring_peer(i), n))
    for i in range(1, CROSS):
        greet((cross_peer(i), n))

    def load(y, x):
        return pltpu.make_async_copy(
            c_ref.at[:, x, y, :], ct.at[y, x, pl.ds(0, S)], load_sem.at[y, x]
        )

    @pl.loop(0, NY)
    def _(y):
        for x in range(NX):
            load(y, x).start()

    smalls = [
        pltpu.make_async_copy(a, b, small_sem.at[i])
        for i, (a, b) in enumerate(
            (
                (heat_ref, heat_v), (spread_ref, spread_v), (fs_ref, vecs[0]), (ft_ref, vecs[1]),
                (fb_ref, vecs[2]), (bs_ref, vecs[3]), (bb_ref, vecs[4]),
                (in_ref, in_v), (out_ref, out_v), (atom_ref, atom_v),
            )
        )
    ]
    lab_copy = pltpu.make_async_copy(lab_ref, lab_v, small_sem.at[10])
    lab_copy.start()
    for c in smalls:
        c.start()

    lab_copy.wait()
    mine[...] = jnp.full((8, 128), -1, I32)
    mine[:, 0:ENTRIES] = jnp.broadcast_to(lab_v[...].reshape(1, ENTRIES), (8, ENTRIES))

    ct[:, :, S:SP, :] = jnp.ones((NY, NX, SP - S, NZ), F32)

    pl.semaphore_wait(barrier, 2 + (NARROW - 1) + (RING - 1) + (CROSS - 1))

    def lab1_copy(i):
        return pltpu.make_async_remote_copy(
            mine, lab1.at[cross], l1s.at[i], l1r.at[i],
            device_id=(cross_peer(i), n), device_id_type=MESH,
        )

    for i in range(1, CROSS):
        lab1_copy(i).start()

    def halo_up(k):
        return pltpu.make_async_remote_copy(
            ct.at[k, :, pl.ds(0, S)], lo.at[k, :, pl.ds(0, S)], hs_sem.at[0, k], hr_sem.at[0, k],
            device_id=(right, n), device_id_type=MESH,
        )

    def halo_down(k):
        return pltpu.make_async_remote_copy(
            ct.at[k, :, pl.ds(0, S)], hi.at[k, :, pl.ds(0, S)], hs_sem.at[1, k], hr_sem.at[1, k],
            device_id=(left, n), device_id_type=MESH,
        )

    @pl.loop(0, EARLY)
    def _(k):
        for x in range(NX):
            load(k, x).wait()
        halo_up(k).start()
        halo_down(k).start()

    @pl.loop(EARLY, NY)
    def _(y):
        for x in range(NX):
            load(y, x).wait()

    lane_e = iota((NX * SP, NZ), 1)
    packed = jnp.zeros((NX * SP, NZ), F32)
    for y in range(NY):
        t = ct[y].reshape(NX * SP, NZ)
        packed = jnp.where(lane_e // 8 == y, pltpu.roll(t, 4 + 8 * y, 1), packed)
    low_half = jnp.bitwise_and(iota((NX * SP // 2, NZ), 1), 7) < 4
    top, bottom = packed[0 : NX * SP // 2], packed[NX * SP // 2 :]
    edge[0] = jnp.where(low_half, top, pltpu.roll(bottom, 4, 1))
    edge[1] = jnp.where(low_half, pltpu.roll(top, NZ - 4, 1), bottom)

    for c in smalls:
        c.wait()
    infull[...] = jnp.zeros((128, RK), F32)
    outfull[...] = jnp.zeros((128, RK), F32)
    atomf[...] = jnp.zeros((8, 128), F32)
    infull[0:S, 0:R] = in_v[...].astype(F32)
    outfull[0:S, 0:R] = out_v[...].astype(F32)
    atomf[0:E, 0:S] = atom_v[...].astype(F32)
    spread[...] = jnp.zeros((8, 128), F32)
    spread[:, 0:S] = jnp.broadcast_to(spread_v[...], (8, S))
    sums[...] = jnp.zeros((RK, 128), F32)

    def edge_right():
        return pltpu.make_async_remote_copy(
            edge.at[0], edge_l, es.at[0], er.at[0], device_id=(w, narrow_peer(1)), device_id_type=MESH
        )

    def edge_left():
        return pltpu.make_async_remote_copy(
            edge.at[1], edge_r, es.at[1], er.at[1],
            device_id=(w, narrow_peer(NARROW - 1)), device_id_type=MESH,
        )

    edge_right().start()
    edge_left().start()

    net_t = outfull[0:64] - infull[0:64]
    fin = jnp.transpose(infull[...])
    fout = jnp.transpose(outfull[...])
    net[:, 0:RK] = net_t.astype(BF16)
    net[:, RK : 2 * RK] = net_t.astype(BF16)

    sub = iota((8, RK), 0)
    vecrows[...] = jnp.zeros((8, RK), F32)
    for k in range(5):
        vecrows[k : k + 1, 0:R] = vecs[k][...].reshape(1, R)
    vec = vecrows[...]
    scale_of = jnp.where((sub == 1), 1.0, LOG2E)
    cols = jnp.transpose(vec * scale_of)
    lane_w = iota((RP, 128), 1)

    def param_lanes(scale, power, barrier_):
        s3 = split3(scale)
        w_ = jnp.zeros((RP, 128), F32)
        vals = [s.astype(F32) for s in s3]
        if power is not None:
            ph, plo = (v.astype(F32) for v in split2(power))
            vals += [ph, plo, ph]
        else:
            vals += [None] * 3
        bh, bl = (v.astype(F32) for v in split2(barrier_))
        vals += [-bh, -bl, -bh]
        for k, v in enumerate(vals):
            if v is not None:
                w_ = jnp.where(lane_w == k, jnp.broadcast_to(v, (RP, 128)), w_)
        return w_.astype(BF16)

    for at, full, power, s, b in ((0, fin, 1, 0, 2), (RP, fout, None, 3, 4)):
        m = full[0:RP]
        weights[at : at + RP, 0:128] = (m + pltpu.roll(m, 64, 1)).astype(BF16)
        weights[at : at + RP, 128:256] = param_lanes(
            cols[0:RP, s : s + 1],
            None if power is None else cols[0:RP, power : power + 1],
            cols[0:RP, b : b + 1],
        )
    rhs[...] = jnp.zeros((256, NX * NZ), BF16)
    rr[...] = jnp.zeros((2 * RK, NX * NZ), BF16)

    gathered = jnp.zeros((8, 128), I32)
    sub8 = iota((8, 128), 0)
    for i in range(1, CROSS):
        lab1_copy(i).wait()
    lab1[cross] = mine[...]
    for i in range(CROSS):
        gathered = jnp.where(sub8 == i, lab1[i], gathered)
    lab2src[...] = gathered
    lab2[ring] = gathered

    def lab2_copy(i):
        return pltpu.make_async_remote_copy(
            lab2src, lab2.at[ring], l2s.at[i], l2r.at[i],
            device_id=(ring_peer(i), n), device_id_type=MESH,
        )

    spread_col = jnp.transpose(jnp.broadcast_to(spread[0:1], (8, 128)))[0:SP, 0:1]
    spread_b = jnp.broadcast_to(spread_col, (SP, NZ)) * (STEP / 5040.0)

    for i in range(1, RING):
        lab2_copy(i).start()

    sub16 = iota((16, NZ), 0)

    @pl.loop(0, NY // 4)
    def _(g):
        acc[...] = jnp.zeros((RP, NX * NZ), F32)
        for k in range(EACH):
            halo_up(EARLY + g * EACH + k).start()
            halo_down(EARLY + g * EACH + k).start()

        @pl.loop(0, 4)
        def _(q):
            y = g * 4 + q

            for x in range(NX):
                zs_ = slice(x * NZ, (x + 1) * NZ)
                logs = jnp.log(ct[y, x]) * LOG2E
                h, l = split2(logs)
                rhs[0:SP, zs_] = h
                rhs[64 : 64 + SP, zs_] = l
                t = heat_v[x, pl.ds(y, 1), :]
                lt_h, lt_l = (v.astype(F32) for v in split2(jnp.log(t) * LOG2E))
                it_h, it_l = (v.astype(F32) for v in split2(1.0 / t))
                p = jnp.where(sub16 < 3, 1.0, 0.0)
                for first, vh, vl in ((3, lt_h, lt_l), (6, it_h, it_l)):
                    p = jnp.where((sub16 == first) | (sub16 == first + 1), jnp.broadcast_to(vh, (16, NZ)), p)
                    p = jnp.where(sub16 == first + 2, jnp.broadcast_to(vl, (16, NZ)), p)
                rhs[128:144, zs_] = p.astype(BF16)
            a = mm(weights[...], rhs[...])
            rates = jnp.exp2(a[0:RP]) - jnp.exp2(a[RP : 2 * RP])
            h, l = split2(rates)
            rr[0:RP] = h
            rr[RK : RK + RP] = l
            acc[...] += rates
            prod = mm(net[...], rr[...])
            for x in range(NX):
                base[y, x] = ct[y, x] + STEP * prod[0:SP, x * NZ : (x + 1) * NZ]

        lane_r = iota((RP, 128), 1)
        cur = sums[0:RP]
        for x in range(NX):
            col = jnp.sum(acc[:, x * NZ : (x + 1) * NZ], axis=1, keepdims=True)
            cur = jnp.where(lane_r == x * 4 + g, jnp.broadcast_to(col, (RP, 128)), cur)
        sums[0:RP] = cur

    rows[pl.ds(pl.multiple_of(n * 16, 16), 16), :] = jnp.transpose(sums[...])[0:16]

    for i in range(1, RING):
        lab2_copy(i).wait()

    labels = lab2[...].reshape(RING * CROSS, 128)
    group = lax.shift_right_arithmetic(labels, 6)
    local = jnp.bitwise_and(labels, 63)
    row_of = jnp.bitwise_and(local, 3) * 16 + lax.shift_right_arithmetic(local, 2)
    wanted = jnp.max(jnp.where(group == w, row_of, -1).astype(F32), axis=1, keepdims=True)
    choose = jnp.where(
        jnp.broadcast_to(wanted, (64, 64)) == iota((64, 64), 1).astype(F32), 1.0, 0.0
    ).astype(BF16)

    def rows_copy(i):
        part = rows.at[pl.ds(pl.multiple_of(n * 16, 16), 16)]
        return pltpu.make_async_remote_copy(
            part, part, ns.at[i], nr.at[i], device_id=(w, narrow_peer(i)), device_id_type=MESH
        )

    def send_halos(first, last):
        @pl.loop(first, last)
        def _(k):
            halo_up(k).start()
            halo_down(k).start()

    for i in range(1, NARROW):
        rows_copy(i).start()
    send_halos(HELD, HELD + ROWS_AFTER)

    a_h = atomf[...].astype(BF16)
    denom = jnp.maximum(mm_t(a_h, fin.astype(BF16)), 1.0)
    dens[...] = 1.0 / denom
    in_b = fin.astype(BF16)
    out_b = fout.astype(BF16)

    @pl.loop(0, PAIRSP // 256)
    def _(t):
        ij = (iota((128, 256), 1) + t * 256).astype(F32)
        i_of = jnp.floor((ij + 0.5) * (1.0 / 53.0))
        j_of = ij - 53.0 * i_of
        want = iota((128, 256), 0).astype(F32)
        r_ = jnp.where(i_of == want, 1.0, 0.0).astype(BF16)
        q_ = jnp.where(j_of == want, 1.0, 0.0).astype(BF16)
        at = pl.ds(pl.multiple_of(t * 256, 256), 256)
        pairs[:, at] = (mm(in_b, r_) * mm(out_b, q_)).astype(BF16)
        afac[:, at] = mm(a_h, r_) * mm(a_h, q_)

    for i in range(1, NARROW):
        rows_copy(i).wait()

    picked3 = split3(rows[...])
    zsend[...] = sum(mm(choose, p) for p in picked3).reshape(RING, CROSS, RK)
    zrecv[ring] = zsend[ring]

    def ring_copy(i):
        to = lax.rem(ring + i, RING)
        return pltpu.make_async_remote_copy(
            zsend.at[to], zrecv.at[ring], zs.at[i], zr.at[i],
            device_id=(ring_peer(i), n), device_id_type=MESH,
        )

    for i in range(1, RING):
        ring_copy(i).start()

    send_halos(HELD + ROWS_AFTER, HELD + ROWS_AFTER + RING_AFTER)


    zi, zo = iota((NZ, NZ), 0), iota((NZ, NZ), 1)
    band = taps_of(zi - zo).astype(BF16)

    @pl.loop(0, NY)
    def _(y):
        c = ct[y].reshape(NX * SP, NZ)
        c_h, c_l = split2(c)
        slot = zi - 8 * y
        at = jnp.where(slot < 4, slot - 4, NZ + slot - 4)
        sides[y] = jnp.where((slot >= 0) & (slot < 8), taps_of(at - zo), 0.0).astype(BF16)
        along = mm(c_h, band) + mm(c_l, band)
        for x in range(NX):
            lap = along[x * SP : (x + 1) * SP] + (3.0 * TAPS[0]) * ct[y, x]
            for k in range(1, 5):
                t = ct[lax.rem(y + k, NY), x] + ct[lax.rem(y + NY - k, NY), x]
                if x + k < NX:
                    t = t + ct[y, x + k]
                if x - k >= 0:
                    t = t + ct[y, x - k]
                lap = lap + TAPS[k] * t
            base[y, x] = base[y, x] + spread_b * lap

    def store(y, x):
        return pltpu.make_async_copy(
            base.at[y, x, pl.ds(0, S)], frac_ref.at[:, x, y, :], store_sem.at[y, x]
        )

    def finish(y):
        halo_up(y).wait()
        halo_down(y).wait()
        for x in range(NX):
            lap = jnp.zeros((SP, NZ), F32)
            for k in range(1, 5):
                if x - k < 0:
                    lap = lap + TAPS[k] * lo[y, NX + x - k]
                if x + k >= NX:
                    lap = lap + TAPS[k] * hi[y, x + k - NX]
            base[y, x] = base[y, x] + spread_b * lap

    @pl.loop(0, READY)
    def _(y):
        finish(y)

    for i in range(1, RING):
        ring_copy(i).wait()

    got = zrecv[...]
    sub_k = iota((8, RK), 0)
    for d in range(CROSS):
        out = jnp.zeros((8, RK), F32)
        for z in range(RING):
            out = jnp.where(sub_k == z, jnp.broadcast_to(got[z, d : d + 1], (8, RK)), out)
        xsend[d] = out
    xrecv[cross] = xsend[cross]

    def cross_copy(i):
        to = lax.rem(cross + i, CROSS)
        return pltpu.make_async_remote_copy(
            xsend.at[to], xrecv.at[cross], xs.at[i], xr.at[i],
            device_id=(cross_peer(i), n), device_id_type=MESH,
        )

    entry_tile = jnp.transpose(jnp.broadcast_to(mine[0:1].astype(F32), (8, 128)))[0:ENTRIES, 0:1]
    group_of = jnp.floor(entry_tile * (1.0 / 64.0))
    pick = jnp.where(
        jnp.broadcast_to(group_of, (ENTRIES, 64)) == iota((ENTRIES, 64), 1).astype(F32), 1.0, 0.0
    ).astype(BF16)

    for i in range(1, CROSS):
        cross_copy(i).start()
    send_halos(HELD + ROWS_AFTER + RING_AFTER, NY)
    edge_right().wait()
    edge_left().wait()
    from_l, from_r = edge_l[...], edge_r[...]
    merged = jnp.concatenate(
        [
            jnp.where(low_half, from_l, pltpu.roll(from_r, 4, 1)),
            jnp.where(low_half, pltpu.roll(from_l, NZ - 4, 1), from_r),
        ],
        axis=0,
    )
    m_h, m_l = split2(merged)

    def close(y):
        beside = mm(m_h, sides[y]) + mm(m_l, sides[y])
        for x in range(NX):
            base[y, x] = base[y, x] + spread_b * beside[x * SP : (x + 1) * SP]
            store(y, x).start()

    @pl.loop(0, READY)
    def _(y):
        close(y)

    for i in range(1, CROSS):
        cross_copy(i).wait()

    picked = sum(mm(pick, p) for p in split3(xrecv[...].reshape(WIDE, RK)))
    scaled = (
        jnp.concatenate(
            [picked * jnp.broadcast_to(dens[k : k + 1], (ENTRIES, RK)) for k in range(E)], axis=0
        )
    )[:, 0:RK]
    s_h, s_l = split2(scaled)
    s_h, s_l = s_h[:, 0:RK], s_l[:, 0:RK]

    for t in range(PAIRSP // 256):
        size = min(256, PAIRS - t * 256)
        at = slice(t * 256, t * 256 + 256)
        v = mm(s_h, pairs[:, at]) + mm(s_l, pairs[:, at])
        for k in range(E):
            f = v[k * ENTRIES : (k + 1) * ENTRIES] * afac[k : k + 1, at]
            flux[k, :, t * 256 : t * 256 + size] = f[:, 0:size]
    flux_copy = pltpu.make_async_copy(flux, flux_ref, flux_sem)
    flux_copy.start()

    @pl.loop(READY, NY)
    def _(y):
        finish(y)
        close(y)

    @pl.loop(0, NY)
    def _(y):
        for x in range(NX):
            store(y, x).wait()

    flux_copy.wait()


def body(
    shares, heat, spread, fs, ft, fb, bs, bb, reactants, products, atoms, labels
):
    any_ = pl.BlockSpec(memory_space=pl.ANY)
    hbm = pl.BlockSpec(memory_space=pltpu.HBM)
    dma = pltpu.SemaphoreType.DMA
    field = pltpu.VMEM((NY, NX, SP, NZ), F32)
    scratch = [
        field, field, field, field,
        pltpu.VMEM((2 * RP, 256), BF16),
        pltpu.VMEM((256, NX * NZ), BF16),
        pltpu.VMEM((2 * RK, NX * NZ), BF16),
        pltpu.VMEM((64, 2 * RK), BF16),
        pltpu.VMEM((RP, NX * NZ), F32),
        pltpu.VMEM((RK, 128), F32),
        pltpu.VMEM((128, RK), F32),
        pltpu.VMEM((128, RK), F32),
        pltpu.VMEM((8, 128), F32),
        pltpu.VMEM((8, 128), F32),
        pltpu.VMEM((8, 128), I32),
        pltpu.VMEM((CROSS, 8, 128), I32),
        pltpu.VMEM((RING, 8, 128), I32),
        pltpu.VMEM((8, 128), I32),
        pltpu.VMEM((2, NX * SP // 2, NZ), F32),
        pltpu.VMEM((NX * SP // 2, NZ), F32),
        pltpu.VMEM((NX * SP // 2, NZ), F32),
        pltpu.VMEM((NY, NZ, NZ), BF16),
        pltpu.VMEM((64, RK), F32),
        pltpu.VMEM((RING, CROSS, RK), F32),
        pltpu.VMEM((RING, CROSS, RK), F32),
        pltpu.VMEM((CROSS, RING, RK), F32),
        pltpu.VMEM((CROSS, RING, RK), F32),
        pltpu.VMEM((RK, PAIRSP), BF16),
        pltpu.VMEM((8, PAIRSP), F32),
        pltpu.VMEM((8, RK), F32),
        pltpu.VMEM((E, ENTRIES, PAIRS), F32),
        pltpu.VMEM((NX, NY, NZ), F32),
        pltpu.VMEM((R,), F32), pltpu.VMEM((R,), F32), pltpu.VMEM((R,), F32), pltpu.VMEM((R,), F32), pltpu.VMEM((R,), F32),
        pltpu.VMEM((8, RK), F32),
        pltpu.VMEM((1, S), F32),
        pltpu.VMEM((S, R), I32),
        pltpu.VMEM((S, R), I32),
        pltpu.VMEM((E, S), I32),
        pltpu.VMEM((ENTRIES,), I32),
        dma((NY, NX)), dma((NY, NX)), dma, dma((2, NY)), dma((2, NY)),
        dma((8,)), dma((8,)), dma((8,)), dma((8,)), dma((2,)), dma((2,)),
        dma((4,)), dma((4,)), dma((8,)), dma((8,)), dma((8,)), dma((8,)), dma((11,)),
    ]
    row = lambda v: v.reshape(1, -1)
    frac, flux = pl.pallas_call(
        kernel,
        out_shape=(
            jax.ShapeDtypeStruct(shares.shape, F32),
            jax.ShapeDtypeStruct((E, ENTRIES, PAIRS), F32),
        ),
        in_specs=[hbm] * 12,
        out_specs=(any_, any_),
        scratch_shapes=scratch,
        compiler_params=pltpu.CompilerParams(
            collective_id=0, has_side_effects=True, vmem_limit_bytes=48 << 20
        ),
    )(
        *(
            pltpu.with_memory_space_constraint(v, pltpu.HBM)
            for v in (
                shares, heat, row(spread), fs, ft, fb, bs, bb, reactants.T, products.T, atoms, labels,
            )
        )
    )
    return frac, jnp.transpose(flux, (1, 0, 2))


def solution(mesh):
    in_specs = (
        P(None, "wide", None, "narrow"), P("wide", None, "narrow"),
        P(), P(), P(), P(), P(), P(), P(), P(), P(), P(("wide", "narrow")),
    )
    out_specs = (P(None, "wide", None, "narrow"), P(("wide", "narrow"), None, None))
    return jax.shard_map(body, mesh=mesh, in_specs=in_specs, out_specs=out_specs, check_vma=False)
```

```python
import functools

import jax
import jax.numpy as jnp
from jax import lax
from jax.experimental import pallas as pl
from jax.experimental.pallas import tpu as pltpu
from jax.sharding import PartitionSpec as P

MESH = pl.DeviceIdType.MESH
F32, BF16, I32 = jnp.float32, jnp.bfloat16, jnp.int32

S, SP = 53, 56
R, RP, RK = 325, 336, 384
PAIRS, PAIRSP = 2809, 2816
E = 5
NX, NY, NZ = 4, 16, 128
WIDE, NARROW = 64, 4
RING, CROSS = 8, 8
ENTRIES = 16
LOG2E = 1.4426950408889634
TAPS = (-14350.0, 8064.0, -1008.0, 128.0, -9.0)
STEP = 0.02
EARLY, EACH, ROWS_AFTER, RING_AFTER = 6, 1, 3, 3
HELD = EARLY + EACH * (NY // 4)
READY = HELD


def split2(v):
    hi = v.astype(BF16)
    return hi, (v - hi.astype(F32)).astype(BF16)


def split3(v):
    hi = v.astype(BF16)
    rest = v - hi.astype(F32)
    mid = rest.astype(BF16)
    return hi, mid, (rest - mid.astype(F32)).astype(BF16)


def iota(shape, dim):
    return lax.broadcasted_iota(I32, shape, dim)


def mm(a, b):
    return jnp.dot(a, b, preferred_element_type=F32)


def mm_t(a, b):
    return lax.dot_general(a, b, (((1,), (1,)), ((), ())), preferred_element_type=F32)


def taps_of(distance):
    w = jnp.zeros(distance.shape, F32)
    for k in range(1, 5):
        w = jnp.where(jnp.abs(distance) == k, TAPS[k], w)
    return w


def kernel(
    c_ref, heat_ref, spread_ref, fs_ref, ft_ref, fb_ref, bs_ref, bb_ref,
    in_ref, out_ref, atom_ref, lab_ref,
    frac_ref, flux_ref,
    ct, lo, hi, base, weights, rhs, rr, net, acc, sums, infull, outfull, atomf,
    spread, mine, lab1, lab2, lab2src, edge, edge_l, edge_r, sides, rows, zsend, zrecv, xsend, xrecv,
    pairs, afac, dens, flux,
    heat_v, v0, v1, v2, v3, v4, vecrows, spread_v, in_v, out_v, atom_v, lab_v,
    load_sem, store_sem, flux_sem, hs_sem, hr_sem, l1s, l1r, l2s, l2r, es, er, ns, nr, zs, zr, xs, xr, small_sem,
):
    vecs = (v0, v1, v2, v3, v4)
    w = lax.axis_index("wide")
    n = lax.axis_index("narrow")
    ring = lax.rem(w, RING)
    cross = w // RING
    right, left = lax.rem(w + 1, WIDE), lax.rem(w + WIDE - 1, WIDE)

    def ring_peer(i):
        return cross * RING + lax.rem(ring + i, RING)

    def cross_peer(i):
        return lax.rem(cross + i, CROSS) * RING + ring

    def narrow_peer(i):
        return lax.rem(n + i, NARROW)

    barrier = pltpu.get_barrier_semaphore()

    def greet(dev):
        pl.semaphore_signal(barrier, inc=1, device_id=dev, device_id_type=MESH)

    greet((right, n))
    greet((left, n))
    for i in range(1, NARROW):
        greet((w, narrow_peer(i)))
    for i in range(1, RING):
        greet((ring_peer(i), n))
    for i in range(1, CROSS):
        greet((cross_peer(i), n))

    def load(y, x):
        return pltpu.make_async_copy(
            c_ref.at[:, x, y, :], ct.at[y, x, pl.ds(0, S)], load_sem.at[y, x]
        )

    @pl.loop(0, NY)
    def _(y):
        for x in range(NX):
            load(y, x).start()

    smalls = [
        pltpu.make_async_copy(a, b, small_sem.at[i])
        for i, (a, b) in enumerate(
            (
                (heat_ref, heat_v), (spread_ref, spread_v), (fs_ref, vecs[0]), (ft_ref, vecs[1]),
                (fb_ref, vecs[2]), (bs_ref, vecs[3]), (bb_ref, vecs[4]),
                (in_ref, in_v), (out_ref, out_v), (atom_ref, atom_v),
            )
        )
    ]
    lab_copy = pltpu.make_async_copy(lab_ref, lab_v, small_sem.at[10])
    lab_copy.start()
    for c in smalls:
        c.start()

    lab_copy.wait()
    mine[...] = jnp.full((8, 128), -1, I32)
    mine[:, 0:ENTRIES] = jnp.broadcast_to(lab_v[...].reshape(1, ENTRIES), (8, ENTRIES))

    ct[:, :, S:SP, :] = jnp.ones((NY, NX, SP - S, NZ), F32)

    pl.semaphore_wait(barrier, 2 + (NARROW - 1) + (RING - 1) + (CROSS - 1))

    def lab1_copy(i):
        return pltpu.make_async_remote_copy(
            mine, lab1.at[cross], l1s.at[i], l1r.at[i],
            device_id=(cross_peer(i), n), device_id_type=MESH,
        )

    for i in range(1, CROSS):
        lab1_copy(i).start()

    def halo_up(k):
        return pltpu.make_async_remote_copy(
            ct.at[k, :, pl.ds(0, S)], lo.at[k, :, pl.ds(0, S)], hs_sem.at[0, k], hr_sem.at[0, k],
            device_id=(right, n), device_id_type=MESH,
        )

    def halo_down(k):
        return pltpu.make_async_remote_copy(
            ct.at[k, :, pl.ds(0, S)], hi.at[k, :, pl.ds(0, S)], hs_sem.at[1, k], hr_sem.at[1, k],
            device_id=(left, n), device_id_type=MESH,
        )

    @pl.loop(0, EARLY)
    def _(k):
        for x in range(NX):
            load(k, x).wait()
        halo_up(k).start()
        halo_down(k).start()

    @pl.loop(EARLY, NY)
    def _(y):
        for x in range(NX):
            load(y, x).wait()

    lane_e = iota((NX * SP, NZ), 1)
    packed = jnp.zeros((NX * SP, NZ), F32)
    for y in range(NY):
        t = ct[y].reshape(NX * SP, NZ)
        packed = jnp.where(lane_e // 8 == y, pltpu.roll(t, 4 + 8 * y, 1), packed)
    low_half = jnp.bitwise_and(iota((NX * SP // 2, NZ), 1), 7) < 4
    top, bottom = packed[0 : NX * SP // 2], packed[NX * SP // 2 :]
    edge[0] = jnp.where(low_half, top, pltpu.roll(bottom, 4, 1))
    edge[1] = jnp.where(low_half, pltpu.roll(top, NZ - 4, 1), bottom)

    for c in smalls:
        c.wait()
    infull[...] = jnp.zeros((128, RK), F32)
    outfull[...] = jnp.zeros((128, RK), F32)
    atomf[...] = jnp.zeros((8, 128), F32)
    infull[0:S, 0:R] = in_v[...].astype(F32)
    outfull[0:S, 0:R] = out_v[...].astype(F32)
    atomf[0:E, 0:S] = atom_v[...].astype(F32)
    spread[...] = jnp.zeros((8, 128), F32)
    spread[:, 0:S] = jnp.broadcast_to(spread_v[...], (8, S))
    sums[...] = jnp.zeros((RK, 128), F32)

    def edge_right():
        return pltpu.make_async_remote_copy(
            edge.at[0], edge_l, es.at[0], er.at[0], device_id=(w, narrow_peer(1)), device_id_type=MESH
        )

    def edge_left():
        return pltpu.make_async_remote_copy(
            edge.at[1], edge_r, es.at[1], er.at[1],
            device_id=(w, narrow_peer(NARROW - 1)), device_id_type=MESH,
        )

    edge_right().start()
    edge_left().start()

    net_t = outfull[0:64] - infull[0:64]
    fin = jnp.transpose(infull[...])
    fout = jnp.transpose(outfull[...])
    net[:, 0:RK] = net_t.astype(BF16)
    net[:, RK : 2 * RK] = net_t.astype(BF16)

    sub = iota((8, RK), 0)
    vecrows[...] = jnp.zeros((8, RK), F32)
    for k in range(5):
        vecrows[k : k + 1, 0:R] = vecs[k][...].reshape(1, R)
    vec = vecrows[...]
    scale_of = jnp.where((sub == 1), 1.0, LOG2E)
    cols = jnp.transpose(vec * scale_of)
    lane_w = iota((RP, 128), 1)

    def param_lanes(scale, power, barrier_):
        s3 = split3(scale)
        w_ = jnp.zeros((RP, 128), F32)
        vals = [s.astype(F32) for s in s3]
        if power is not None:
            ph, plo = (v.astype(F32) for v in split2(power))
            vals += [ph, plo, ph]
        else:
            vals += [None] * 3
        bh, bl = (v.astype(F32) for v in split2(barrier_))
        vals += [-bh, -bl, -bh]
        for k, v in enumerate(vals):
            if v is not None:
                w_ = jnp.where(lane_w == k, jnp.broadcast_to(v, (RP, 128)), w_)
        return w_.astype(BF16)

    for at, full, power, s, b in ((0, fin, 1, 0, 2), (RP, fout, None, 3, 4)):
        m = full[0:RP]
        weights[at : at + RP, 0:128] = (m + pltpu.roll(m, 64, 1)).astype(BF16)
        weights[at : at + RP, 128:256] = param_lanes(
            cols[0:RP, s : s + 1],
            None if power is None else cols[0:RP, power : power + 1],
            cols[0:RP, b : b + 1],
        )
    rhs[...] = jnp.zeros((256, NX * NZ), BF16)
    rr[...] = jnp.zeros((2 * RK, NX * NZ), BF16)

    gathered = jnp.zeros((8, 128), I32)
    sub8 = iota((8, 128), 0)
    for i in range(1, CROSS):
        lab1_copy(i).wait()
    lab1[cross] = mine[...]
    for i in range(CROSS):
        gathered = jnp.where(sub8 == i, lab1[i], gathered)
    lab2src[...] = gathered
    lab2[ring] = gathered

    def lab2_copy(i):
        return pltpu.make_async_remote_copy(
            lab2src, lab2.at[ring], l2s.at[i], l2r.at[i],
            device_id=(ring_peer(i), n), device_id_type=MESH,
        )

    spread_col = jnp.transpose(jnp.broadcast_to(spread[0:1], (8, 128)))[0:SP, 0:1]
    spread_b = jnp.broadcast_to(spread_col, (SP, NZ)) * (STEP / 5040.0)

    for i in range(1, RING):
        lab2_copy(i).start()

    sub16 = iota((16, NZ), 0)

    @pl.loop(0, NY // 4)
    def _(g):
        acc[...] = jnp.zeros((RP, NX * NZ), F32)
        for k in range(EACH):
            halo_up(EARLY + g * EACH + k).start()
            halo_down(EARLY + g * EACH + k).start()

        @pl.loop(0, 4)
        def _(q):
            y = g * 4 + q

            for x in range(NX):
                zs_ = slice(x * NZ, (x + 1) * NZ)
                logs = jnp.log(ct[y, x]) * LOG2E
                h, l = split2(logs)
                rhs[0:SP, zs_] = h
                rhs[64 : 64 + SP, zs_] = l
                t = heat_v[x, pl.ds(y, 1), :]
                lt_h, lt_l = (v.astype(F32) for v in split2(jnp.log(t) * LOG2E))
                it_h, it_l = (v.astype(F32) for v in split2(1.0 / t))
                p = jnp.where(sub16 < 3, 1.0, 0.0)
                for first, vh, vl in ((3, lt_h, lt_l), (6, it_h, it_l)):
                    p = jnp.where((sub16 == first) | (sub16 == first + 1), jnp.broadcast_to(vh, (16, NZ)), p)
                    p = jnp.where(sub16 == first + 2, jnp.broadcast_to(vl, (16, NZ)), p)
                rhs[128:144, zs_] = p.astype(BF16)
            a = mm(weights[...], rhs[...])
            rates = jnp.exp2(a[0:RP]) - jnp.exp2(a[RP : 2 * RP])
            h, l = split2(rates)
            rr[0:RP] = h
            rr[RK : RK + RP] = l
            acc[...] += rates
            prod = mm(net[...], rr[...])
            for x in range(NX):
                base[y, x] = ct[y, x] + STEP * prod[0:SP, x * NZ : (x + 1) * NZ]

        lane_r = iota((RP, 128), 1)
        cur = sums[0:RP]
        for x in range(NX):
            col = jnp.sum(acc[:, x * NZ : (x + 1) * NZ], axis=1, keepdims=True)
            cur = jnp.where(lane_r == x * 4 + g, jnp.broadcast_to(col, (RP, 128)), cur)
        sums[0:RP] = cur

    rows[pl.ds(pl.multiple_of(n * 16, 16), 16), :] = jnp.transpose(sums[...])[0:16]

    for i in range(1, RING):
        lab2_copy(i).wait()

    labels = lab2[...].reshape(RING * CROSS, 128)
    group = lax.shift_right_arithmetic(labels, 6)
    local = jnp.bitwise_and(labels, 63)
    row_of = jnp.bitwise_and(local, 3) * 16 + lax.shift_right_arithmetic(local, 2)
    wanted = jnp.max(jnp.where(group == w, row_of, -1).astype(F32), axis=1, keepdims=True)
    choose = jnp.where(
        jnp.broadcast_to(wanted, (64, 64)) == iota((64, 64), 1).astype(F32), 1.0, 0.0
    ).astype(BF16)

    def rows_copy(i):
        part = rows.at[pl.ds(pl.multiple_of(n * 16, 16), 16)]
        return pltpu.make_async_remote_copy(
            part, part, ns.at[i], nr.at[i], device_id=(w, narrow_peer(i)), device_id_type=MESH
        )

    def send_halos(first, last):
        @pl.loop(first, last)
        def _(k):
            halo_up(k).start()
            halo_down(k).start()

    for i in range(1, NARROW):
        rows_copy(i).start()
    send_halos(HELD, HELD + ROWS_AFTER)

    a_h = atomf[...].astype(BF16)
    denom = jnp.maximum(mm_t(a_h, fin.astype(BF16)), 1.0)
    dens[...] = 1.0 / denom
    in_b = fin.astype(BF16)
    out_b = fout.astype(BF16)

    @pl.loop(0, PAIRSP // 256)
    def _(t):
        ij = (iota((128, 256), 1) + t * 256).astype(F32)
        i_of = jnp.floor((ij + 0.5) * (1.0 / 53.0))
        j_of = ij - 53.0 * i_of
        want = iota((128, 256), 0).astype(F32)
        r_ = jnp.where(i_of == want, 1.0, 0.0).astype(BF16)
        q_ = jnp.where(j_of == want, 1.0, 0.0).astype(BF16)
        at = pl.ds(pl.multiple_of(t * 256, 256), 256)
        pairs[:, at] = (mm(in_b, r_) * mm(out_b, q_)).astype(BF16)
        afac[:, at] = mm(a_h, r_) * mm(a_h, q_)

    for i in range(1, NARROW):
        rows_copy(i).wait()

    picked3 = split3(rows[...])
    zsend[...] = sum(mm(choose, p) for p in picked3).reshape(RING, CROSS, RK)
    zrecv[ring] = zsend[ring]

    def ring_copy(i):
        to = lax.rem(ring + i, RING)
        return pltpu.make_async_remote_copy(
            zsend.at[to], zrecv.at[ring], zs.at[i], zr.at[i],
            device_id=(ring_peer(i), n), device_id_type=MESH,
        )

    for i in range(1, RING):
        ring_copy(i).start()

    send_halos(HELD + ROWS_AFTER, HELD + ROWS_AFTER + RING_AFTER)


    zi, zo = iota((NZ, NZ), 0), iota((NZ, NZ), 1)
    band = taps_of(zi - zo).astype(BF16)

    @pl.loop(0, NY)
    def _(y):
        c = ct[y].reshape(NX * SP, NZ)
        c_h, c_l = split2(c)
        slot = zi - 8 * y
        at = jnp.where(slot < 4, slot - 4, NZ + slot - 4)
        sides[y] = jnp.where((slot >= 0) & (slot < 8), taps_of(at - zo), 0.0).astype(BF16)
        along = mm(c_h, band) + mm(c_l, band)
        for x in range(NX):
            lap = along[x * SP : (x + 1) * SP] + (3.0 * TAPS[0]) * ct[y, x]
            for k in range(1, 5):
                t = ct[lax.rem(y + k, NY), x] + ct[lax.rem(y + NY - k, NY), x]
                if x + k < NX:
                    t = t + ct[y, x + k]
                if x - k >= 0:
                    t = t + ct[y, x - k]
                lap = lap + TAPS[k] * t
            base[y, x] = base[y, x] + spread_b * lap

    def store(y, x):
        return pltpu.make_async_copy(
            base.at[y, x, pl.ds(0, S)], frac_ref.at[:, x, y, :], store_sem.at[y, x]
        )

    def finish(y):
        halo_up(y).wait()
        halo_down(y).wait()
        for x in range(NX):
            lap = jnp.zeros((SP, NZ), F32)
            for k in range(1, 5):
                if x - k < 0:
                    lap = lap + TAPS[k] * lo[y, NX + x - k]
                if x + k >= NX:
                    lap = lap + TAPS[k] * hi[y, x + k - NX]
            base[y, x] = base[y, x] + spread_b * lap

    @pl.loop(0, READY)
    def _(y):
        finish(y)

    for i in range(1, RING):
        ring_copy(i).wait()

    got = zrecv[...]
    sub_k = iota((8, RK), 0)
    for d in range(CROSS):
        out = jnp.zeros((8, RK), F32)
        for z in range(RING):
            out = jnp.where(sub_k == z, jnp.broadcast_to(got[z, d : d + 1], (8, RK)), out)
        xsend[d] = out
    xrecv[cross] = xsend[cross]

    def cross_copy(i):
        to = lax.rem(cross + i, CROSS)
        return pltpu.make_async_remote_copy(
            xsend.at[to], xrecv.at[cross], xs.at[i], xr.at[i],
            device_id=(cross_peer(i), n), device_id_type=MESH,
        )

    entry_tile = jnp.transpose(jnp.broadcast_to(mine[0:1].astype(F32), (8, 128)))[0:ENTRIES, 0:1]
    group_of = jnp.floor(entry_tile * (1.0 / 64.0))
    pick = jnp.where(
        jnp.broadcast_to(group_of, (ENTRIES, 64)) == iota((ENTRIES, 64), 1).astype(F32), 1.0, 0.0
    ).astype(BF16)

    for i in range(1, CROSS):
        cross_copy(i).start()
    send_halos(HELD + ROWS_AFTER + RING_AFTER, NY)
    edge_right().wait()
    edge_left().wait()
    from_l, from_r = edge_l[...], edge_r[...]
    merged = jnp.concatenate(
        [
            jnp.where(low_half, from_l, pltpu.roll(from_r, 4, 1)),
            jnp.where(low_half, pltpu.roll(from_l, NZ - 4, 1), from_r),
        ],
        axis=0,
    )
    m_h, m_l = split2(merged)

    def close(y):
        beside = mm(m_h, sides[y]) + mm(m_l, sides[y])
        for x in range(NX):
            base[y, x] = base[y, x] + spread_b * beside[x * SP : (x + 1) * SP]
            store(y, x).start()

    @pl.loop(0, READY)
    def _(y):
        close(y)

    @pl.loop(READY, NY)
    def _(y):
        finish(y)
        close(y)

    for i in range(1, CROSS):
        cross_copy(i).wait()

    picked = sum(mm(pick, p) for p in split3(xrecv[...].reshape(WIDE, RK)))
    scaled = (
        jnp.concatenate(
            [picked * jnp.broadcast_to(dens[k : k + 1], (ENTRIES, RK)) for k in range(E)], axis=0
        )
    )[:, 0:RK]
    s_h, s_l = split2(scaled)
    s_h, s_l = s_h[:, 0:RK], s_l[:, 0:RK]

    for t in range(PAIRSP // 256):
        size = min(256, PAIRS - t * 256)
        at = slice(t * 256, t * 256 + 256)
        v = mm(s_h, pairs[:, at]) + mm(s_l, pairs[:, at])
        for k in range(E):
            f = v[k * ENTRIES : (k + 1) * ENTRIES] * afac[k : k + 1, at]
            flux[k, :, t * 256 : t * 256 + size] = f[:, 0:size]
    flux_copy = pltpu.make_async_copy(flux, flux_ref, flux_sem)
    flux_copy.start()


    @pl.loop(0, NY)
    def _(y):
        for x in range(NX):
            store(y, x).wait()

    flux_copy.wait()


def body(
    shares, heat, spread, fs, ft, fb, bs, bb, reactants, products, atoms, labels
):
    any_ = pl.BlockSpec(memory_space=pl.ANY)
    hbm = pl.BlockSpec(memory_space=pltpu.HBM)
    dma = pltpu.SemaphoreType.DMA
    field = pltpu.VMEM((NY, NX, SP, NZ), F32)
    scratch = [
        field, field, field, field,
        pltpu.VMEM((2 * RP, 256), BF16),
        pltpu.VMEM((256, NX * NZ), BF16),
        pltpu.VMEM((2 * RK, NX * NZ), BF16),
        pltpu.VMEM((64, 2 * RK), BF16),
        pltpu.VMEM((RP, NX * NZ), F32),
        pltpu.VMEM((RK, 128), F32),
        pltpu.VMEM((128, RK), F32),
        pltpu.VMEM((128, RK), F32),
        pltpu.VMEM((8, 128), F32),
        pltpu.VMEM((8, 128), F32),
        pltpu.VMEM((8, 128), I32),
        pltpu.VMEM((CROSS, 8, 128), I32),
        pltpu.VMEM((RING, 8, 128), I32),
        pltpu.VMEM((8, 128), I32),
        pltpu.VMEM((2, NX * SP // 2, NZ), F32),
        pltpu.VMEM((NX * SP // 2, NZ), F32),
        pltpu.VMEM((NX * SP // 2, NZ), F32),
        pltpu.VMEM((NY, NZ, NZ), BF16),
        pltpu.VMEM((64, RK), F32),
        pltpu.VMEM((RING, CROSS, RK), F32),
        pltpu.VMEM((RING, CROSS, RK), F32),
        pltpu.VMEM((CROSS, RING, RK), F32),
        pltpu.VMEM((CROSS, RING, RK), F32),
        pltpu.VMEM((RK, PAIRSP), BF16),
        pltpu.VMEM((8, PAIRSP), F32),
        pltpu.VMEM((8, RK), F32),
        pltpu.VMEM((E, ENTRIES, PAIRS), F32),
        pltpu.VMEM((NX, NY, NZ), F32),
        pltpu.VMEM((R,), F32), pltpu.VMEM((R,), F32), pltpu.VMEM((R,), F32), pltpu.VMEM((R,), F32), pltpu.VMEM((R,), F32),
        pltpu.VMEM((8, RK), F32),
        pltpu.VMEM((1, S), F32),
        pltpu.VMEM((S, R), I32),
        pltpu.VMEM((S, R), I32),
        pltpu.VMEM((E, S), I32),
        pltpu.VMEM((ENTRIES,), I32),
        dma((NY, NX)), dma((NY, NX)), dma, dma((2, NY)), dma((2, NY)),
        dma((8,)), dma((8,)), dma((8,)), dma((8,)), dma((2,)), dma((2,)),
        dma((4,)), dma((4,)), dma((8,)), dma((8,)), dma((8,)), dma((8,)), dma((11,)),
    ]
    row = lambda v: v.reshape(1, -1)
    frac, flux = pl.pallas_call(
        kernel,
        out_shape=(
            jax.ShapeDtypeStruct(shares.shape, F32),
            jax.ShapeDtypeStruct((E, ENTRIES, PAIRS), F32),
        ),
        in_specs=[hbm] * 12,
        out_specs=(any_, any_),
        scratch_shapes=scratch,
        compiler_params=pltpu.CompilerParams(
            collective_id=0, has_side_effects=True, vmem_limit_bytes=48 << 20
        ),
    )(
        *(
            pltpu.with_memory_space_constraint(v, pltpu.HBM)
            for v in (
                shares, heat, row(spread), fs, ft, fb, bs, bb, reactants.T, products.T, atoms, labels,
            )
        )
    )
    return frac, jnp.transpose(flux, (1, 0, 2))


def solution(mesh):
    in_specs = (
        P(None, "wide", None, "narrow"), P("wide", None, "narrow"),
        P(), P(), P(), P(), P(), P(), P(), P(), P(), P(("wide", "narrow")),
    )
    out_specs = (P(None, "wide", None, "narrow"), P(("wide", "narrow"), None, None))
    return jax.shard_map(body, mesh=mesh, in_specs=in_specs, out_specs=out_specs, check_vma=False)
```
